32 devices in a mesh: fsdp: 8 (over z, y), seq: 4 (over x, core).
Axes of the slice: x: 2, y: 2, z: 4, core: 2. Of those that a mesh axis runs over, the one named last changes fastest.
Arguments:
- decoder_layer_input: bfloat16 [16, 1024, 2048], P('fsdp', 'seq'), may hold values from -6 to 6
- lengths: int32 [16], P('fsdp'), may hold values from 256 to 1024, as said below
- ln1_gain: bfloat16 [2048], P('fsdp'), may hold values from 0.5 to 1.5
- ln1_bias: bfloat16 [2048], P('fsdp'), may hold values from -1.1953125 to 1.1953125
- qkv_weight: bfloat16 [2048, 6144], P('fsdp'), may hold values from -0.125 to 0.125
- qkv_bias: bfloat16 [6144], P('fsdp'), may hold values from -1.796875 to 1.796875
- out_weight: bfloat16 [2048, 2048], P('fsdp'), may hold values from -2 to 2
- ln2_gain: bfloat16 [2048], P('fsdp'), may hold values from 0.5 to 1.5
- ln2_bias: bfloat16 [2048], P('fsdp'), may hold values from -1.1953125 to 1.1953125
- gate_weight: bfloat16 [2048, 5632], P('fsdp'), may hold values from -0.125 to 0.125
- up_weight: bfloat16 [2048, 5632], P('fsdp'), may hold values from -0.125 to 0.125
- down_weight: bfloat16 [5632, 2048], P('fsdp'), may hold values from -0.078125 to 0.078125
- cotangent: bfloat16 [16, 1024, 2048], P('fsdp', 'seq'), may hold values from -6 to 6
Outputs:
- layer_output: bfloat16 [16, 1024, 2048], P('fsdp', 'seq')
- grad_x: float32 [16, 1024, 2048], P('fsdp', 'seq')
- grad_ln1_gain: float32 [2048], P('fsdp')
- grad_ln1_bias: float32 [2048], P('fsdp')
- grad_qkv_weight: float32 [2048, 6144], P('fsdp')
- grad_qkv_bias: float32 [6144], P('fsdp')
- grad_out_weight: float32 [2048, 2048], P('fsdp')
- grad_ln2_gain: float32 [2048], P('fsdp')
- grad_ln2_bias: float32 [2048], P('fsdp')
- grad_gate_weight: float32 [2048, 5632], P('fsdp')
- grad_up_weight: float32 [2048, 5632], P('fsdp')
- grad_down_weight: float32 [5632, 2048], P('fsdp')
The draws below stay inside these ranges and needn't reach their ends.
Inputs may be any that keep to these rules, and one draw needn't show every extreme that they name: `lengths`: each slot's count of valid positions; in every draw some slot is full with 1024.
All inputs are finite; a program needn't handle non-finite values.
Results may differ from the reference program's by a relative error of at most 0.018.
Values may be sent and summed in bfloat16 or wider, within the bound.
No kernel may reach another device: no remote copies, remote signals or barrier semaphores. Data moves between devices by JAX's collectives and lax.ppermute only.
A program may use at most 512 MiB of HBM per device.

```python
import jax
import jax.numpy as jnp
from jax import lax

D = 2048
FF = 5632
HEADS = 32
HEAD_DIM = 64
ROT = 16
SLOT = 1024
SLOTS = 16


def draw_lengths(key, part):
    key_one, key_two = jax.random.split(key)
    drawn = jax.random.randint(key_one, (SLOTS,), SLOT // 4, SLOT + 1)
    chosen = jax.random.randint(key_two, (), 0, SLOTS)
    return jnp.where(jnp.arange(SLOTS) == chosen, SLOT, drawn).astype(jnp.int32)


def block_scale(key, dims, cuts, smallest, largest):
    factor_of, own = 1.0, jax.random.fold_in(key, 6)
    for axis_at, shards_of in cuts:
        heights = jnp.exp(jax.random.uniform(jax.random.fold_in(own, axis_at), (shards_of,), jnp.float32, smallest / len(cuts), largest / len(cuts)))
        factor_of = factor_of * jnp.repeat(heights, dims[axis_at] // shards_of).reshape([-1 if axis == axis_at else 1 for axis in range(len(dims))])
    return factor_of


def centred(rng, shape, scale, limit, cuts=(), held_as=jnp.bfloat16):
    gain = block_scale(rng, shape, cuts, -0.22, 0.18) if cuts else 1.0
    array = jax.random.normal(rng, shape, jnp.float32) * scale * gain
    return jnp.minimum(jnp.maximum(array, -limit), limit).astype(held_as)


def setup_inputs(seed: int = 0) -> dict:
    arg_keys = jax.random.split(jax.random.key(seed), 14)
    decoder_layer_input = centred(arg_keys[0], (SLOTS, SLOT, D), 1.0, 6.0, ((0, 8), (1, 4)))
    lengths = draw_lengths(jax.random.fold_in(arg_keys[13], 71), 0)
    ln1_gain = jnp.clip(1.0 + 0.1 * jax.random.normal(arg_keys[2], (D,), jnp.float32), 0.5, 1.5).astype(jnp.bfloat16)
    ln1_bias = centred(arg_keys[3], (D,), 0.2, 1.1953125, ((0, 8),))
    qkv_weight = centred(arg_keys[4], (D, 3 * D), D ** -0.5, 0.125, ((0, 8),))
    qkv_bias = centred(arg_keys[5], (3 * D,), 0.3, 1.796875, ((0, 8),))
    out_weight = centred(arg_keys[6], (D, D), (max(D // 256, 1)) ** -0.5, 2.0, ((0, 8),))
    ln2_gain = jnp.clip(1.0 + 0.1 * jax.random.normal(arg_keys[7], (D,), jnp.float32), 0.5, 1.5).astype(jnp.bfloat16)
    ln2_bias = centred(arg_keys[8], (D,), 0.2, 1.1953125, ((0, 8),))
    gate_weight = centred(arg_keys[9], (D, FF), D ** -0.5, 0.125, ((0, 8),))
    up_weight = centred(arg_keys[10], (D, FF), D ** -0.5, 0.125, ((0, 8),))
    down_weight = centred(arg_keys[11], (FF, D), FF ** -0.5, 0.078125, ((0, 8),))
    cotangent = centred(arg_keys[12], (SLOTS, SLOT, D), 1.0, 6.0, ((0, 8), (1, 4)))
    return dict(decoder_layer_input=decoder_layer_input, lengths=lengths, ln1_gain=ln1_gain, ln1_bias=ln1_bias, qkv_weight=qkv_weight, qkv_bias=qkv_bias, out_weight=out_weight, ln2_gain=ln2_gain, ln2_bias=ln2_bias, gate_weight=gate_weight, up_weight=up_weight, down_weight=down_weight, cotangent=cotangent)


@jax.custom_vjp
def low(v):
    return lax.optimization_barrier(v.astype(jnp.bfloat16)).astype(jnp.float32)

@jax.custom_vjp
def low_back(v):
    return v

def low_keep(v):
    return (low(v), None)

def low_pass(kept, grad):
    return (grad,)

def back_keep(v):
    return (v, None)

def back_low(kept, grad):
    return (low(grad),)
low.defvjp(low_keep, low_pass)
low_back.defvjp(back_keep, back_low)
EPS_NORM = 1e-05
ROPE_BASE = 10000.0
NEG_FILL = -1e+30

def layer_norm(values, gain_vec, shift_vec):
    center = values - lax.optimization_barrier(jnp.mean(values, axis=-1, keepdims=True))
    scaled = center * lax.rsqrt(lax.optimization_barrier(jnp.mean(center * center, axis=-1, keepdims=True)) + EPS_NORM)
    return scaled * gain_vec + shift_vec

def rotary(values, cosine, sine_table):
    half_rot = ROT // 2
    front_half = values[..., :half_rot]
    back_half = values[..., half_rot:ROT]
    return jnp.concatenate([front_half * cosine - back_half * sine_table, back_half * cosine + front_half * sine_table, values[..., ROT:]], axis=-1)

def tables(position):
    inverse = ROPE_BASE ** (-(jnp.arange(ROT // 2).astype(jnp.float32) * 2.0) / ROT)
    angles = position[:, None] * inverse[None, :]
    return (jnp.cos(angles)[:, None, :], jnp.sin(angles)[:, None, :])

def matmul(left_operand, right_operand):
    return jnp.einsum('wjg,gb->wjb', left_operand, right_operand, precision=lax.Precision.HIGHEST)

def reference(decoder_layer_input, lengths, ln1_gain, ln1_bias, qkv_weight, qkv_bias, out_weight, ln2_gain, ln2_bias, gate_weight, up_weight, down_weight, cotangent):
    params = tuple((item.astype(jnp.float32) for item in (ln1_gain, ln1_bias, qkv_weight, qkv_bias, out_weight, ln2_gain, ln2_bias, gate_weight, up_weight, down_weight)))
    position = jnp.arange(SLOT).astype(jnp.float32)
    cosine, sine_table = tables(position)
    slot_pos = jnp.arange(SLOT).astype(jnp.int32)
    scale = HEAD_DIM ** (-0.5)

    def attend(inputs):
        query_rows, key_rows, value_rows, seq_limit = inputs
        scores = low_back(jnp.einsum('qhd,khd->hqk', query_rows, key_rows, precision=lax.Precision.HIGHEST) * scale)
        allowed = (slot_pos[None, :] <= slot_pos[:, None]) & (slot_pos[None, :] < seq_limit)
        scores = jnp.where(allowed[None], scores, NEG_FILL)
        row_peak = lax.optimization_barrier(jnp.max(scores, axis=-1, keepdims=True))
        exp_scores = jnp.exp(scores - row_peak)
        probability_rows = low(exp_scores / lax.optimization_barrier(jnp.sum(exp_scores, axis=-1, keepdims=True)))
        return jnp.einsum('hqk,khd->qhd', probability_rows, value_rows, precision=lax.Precision.HIGHEST).reshape(SLOT, D)

    def forward_pass(tokens_in, norm1_gain, norm1_shift, qkv_full, qkv_shift, out_full, norm2_gain, norm2_shift, gate_full, up_full, down_full):
        normed = low(layer_norm(tokens_in, norm1_gain, norm1_shift))
        projected = low_back(matmul(normed, qkv_full) + qkv_shift)
        shaped = projected.reshape(SLOTS, SLOT, 3, HEADS, HEAD_DIM)
        query_rows = rotary(shaped[:, :, 0], cosine, sine_table)
        key_rows = rotary(shaped[:, :, 1], cosine, sine_table)
        stacked = low(low_back(jnp.stack([query_rows, key_rows, shaped[:, :, 2]], axis=2)))
        attended = lax.map(jax.checkpoint(attend), (stacked[:, :, 0], stacked[:, :, 1], stacked[:, :, 2], lengths))
        merged = low(low_back(attended))
        residual = tokens_in + low_back(matmul(merged, out_full))
        normed_two = low(layer_norm(residual, norm2_gain, norm2_shift))
        gate_val = low_back(matmul(normed_two, gate_full))
        up_val = low_back(matmul(normed_two, up_full))
        hidden = low(jax.nn.silu(gate_val) * up_val)
        return residual + matmul(hidden, down_full)
    valid_rows = (slot_pos[None, :] < lengths[:, None]).astype(jnp.float32)
    result, pull_back = jax.vjp(forward_pass, decoder_layer_input.astype(jnp.float32), *params)
    grads = pull_back(cotangent.astype(jnp.float32) * valid_rows[:, :, None])
    return (result.astype(jnp.bfloat16), grads[0], grads[1], grads[2], grads[3], grads[4], grads[5], grads[6], grads[7], grads[8], grads[9], grads[10])
```

```python
import jax
import jax.numpy as jnp
from jax import lax
from jax.sharding import PartitionSpec as P

HEAD_DIM = 64
ROT = 16
EPS_NORM = 1e-05
ROPE_BASE = 10000.0
NEG_FILL = -1e30
BF = jnp.bfloat16
F32 = jnp.float32


def dot(a, b, ca, cb):
    return lax.dot_general(a, b, (((ca,), (cb,)), ((), ())), preferred_element_type=F32)


def norm_stats(v):
    center = v - jnp.mean(v, axis=-1, keepdims=True)
    rstd = lax.rsqrt(jnp.mean(center * center, axis=-1, keepdims=True) + EPS_NORM)
    return center * rstd, rstd


def norm_back(grad, xhat, rstd, gain):
    gx = grad * gain
    m1 = jnp.mean(gx, axis=-1, keepdims=True)
    m2 = jnp.mean(gx * xhat, axis=-1, keepdims=True)
    return (gx - m1 - xhat * m2) * rstd


class SeqGroup:
    def __init__(self, size):
        self.size = size
        self.me = lax.axis_index("seq")
        self.offsets = (0, 2, 1, 3) if size == 4 else tuple(range(size))

    def place(self, j):
        return self.me ^ self.offsets[j] if self.size == 4 else jnp.int32(j)

    def swap(self, v, bit):
        return lax.ppermute(v, "seq", [(i, i ^ bit) for i in range(self.size)])

    def gather(self, v):
        if self.size != 4:
            return list(lax.all_gather(v, "seq", axis=0))
        far = self.swap(v, 2)
        return [v, far, self.swap(v, 1), self.swap(far, 1)]

    def scatter(self, part):
        if self.size != 4:
            terms = jnp.stack([part(j).astype(BF) for j in range(self.size)])
            return lax.psum_scatter(terms, "seq", scatter_dimension=0).astype(F32)
        diag = self.swap(part(3).astype(BF), 1)
        far = self.swap((part(1) + diag.astype(F32)).astype(BF), 2)
        near = self.swap(part(2).astype(BF), 1)
        return part(0) + near.astype(F32) + far.astype(F32)

    def gather_placed(self, v):
        blocks = self.gather(v)
        if self.size != 4:
            return jnp.stack(blocks)
        low = (self.me & 1) == 0
        high = (self.me & 2) == 0
        a, c, b, d = blocks
        first = [jnp.where(low, a, b), jnp.where(low, b, a)]
        second = [jnp.where(low, c, d), jnp.where(low, d, c)]
        return jnp.stack(
            [jnp.where(high, x, y) for x, y in zip(first, second)]
            + [jnp.where(high, y, x) for x, y in zip(first, second)]
        )


def rope(v, cosine, sine):
    h = ROT // 2
    a, b = v[..., :h], v[..., h:ROT]
    return jnp.concatenate([a * cosine - b * sine, b * cosine + a * sine, v[..., ROT:]], axis=-1)


def scores_of(q, k, start, limit):
    sc = jnp.einsum("qhd,khd->hqk", q, k, preferred_element_type=F32) * HEAD_DIM**-0.5
    row = start + jnp.arange(q.shape[0])
    col = jnp.arange(k.shape[0])
    ok = (col[None, :] <= row[:, None]) & (col[None, :] < limit)
    return jnp.where(ok[None], sc, NEG_FILL)


def attend(q, k, v, limit):
    n = q.shape[0] // 2
    outs, lses = [], []
    for i in range(2):
        sc = scores_of(q[i * n : (i + 1) * n], k[: (i + 1) * n], i * n, limit)
        peak = jnp.max(sc, axis=-1, keepdims=True)
        e = jnp.exp(sc - peak)
        tot = jnp.sum(e, axis=-1, keepdims=True)
        outs.append(jnp.einsum("hqk,khd->qhd", (e / tot).astype(BF), v[: (i + 1) * n], preferred_element_type=F32))
        lses.append(peak[..., 0] + jnp.log(tot[..., 0]))
    return jnp.concatenate(outs, axis=0), lses


def attend_back(q, k, v, limit, lses, g):
    n = q.shape[0] // 2
    scale = HEAD_DIM**-0.5
    dqs = []
    dk = jnp.zeros(k.shape, F32)
    dv = jnp.zeros(v.shape, F32)
    for i in range(2):
        m = (i + 1) * n
        qi, gi = q[i * n : m], g[i * n : m]
        p = jnp.exp(scores_of(qi, k[:m], i * n, limit) - lses[i][..., None])
        gp = jnp.einsum("qhd,khd->hqk", gi, v[:m], preferred_element_type=F32)
        ds = (p * (gp - jnp.sum(p * gp, axis=-1, keepdims=True))).astype(BF)
        dqs.append(jnp.einsum("hqk,khd->qhd", ds, k[:m], preferred_element_type=F32) * scale)
        dk = dk.at[:m].add(jnp.einsum("hqk,qhd->khd", ds, qi, preferred_element_type=F32) * scale)
        dv = dv.at[:m].add(jnp.einsum("hqk,qhd->khd", p.astype(BF), gi, preferred_element_type=F32))
    return jnp.concatenate(dqs, axis=0), dk, dv


def body(
    x_in, lengths, ln1_gain, ln1_bias, qkv_weight, qkv_bias, out_weight,
    ln2_gain, ln2_bias, gate_weight, up_weight, down_weight, cotangent,
):
    nf, ns = lax.axis_size("fsdp"), lax.axis_size("seq")
    seq = SeqGroup(ns)
    me = seq.me
    slots, pos, d = x_in.shape
    rows = qkv_weight.shape[0]
    heads = qkv_weight.shape[1] // (3 * HEAD_DIM)
    mine = heads // ns
    tok = slots * pos
    ff = gate_weight.shape[1]
    unit = ff // (nf * ns)
    spread = (heads // nf) % ns == 0

    def pick(v, groups, width):
        v = v.reshape(v.shape[0], groups, ns, width)
        v = lax.dynamic_index_in_dim(v, me, axis=2, keepdims=False)
        return v.reshape(v.shape[0], groups * width)

    def unpick(pieces, groups, width):
        v = pieces.reshape(ns, pieces.shape[1], groups, width)
        return jnp.moveaxis(v, 0, 2).reshape(pieces.shape[1], groups * ns * width)

    def pick_rows(v):
        return lax.dynamic_index_in_dim(v.reshape(ns, v.shape[0] // ns, v.shape[1]), me, 0, keepdims=False)

    def collect(v):
        return lax.all_gather(v, "fsdp", axis=0, tiled=True)

    def reduce(v):
        return lax.psum_scatter(v, "fsdp", scatter_dimension=0, tiled=True)

    qgroups, qwidth = (3 * nf, mine * HEAD_DIM // nf) if spread else (3, mine * HEAD_DIM)

    small = collect(jnp.concatenate([ln1_gain, ln1_bias, ln2_gain, ln2_bias, qkv_bias])[None])
    gain1, bias1, gain2, bias2 = (small[:, i * rows : (i + 1) * rows].reshape(d).astype(F32) for i in range(4))
    bias_q = pick(small[:, 4 * rows :].reshape(1, -1), qgroups, qwidth).astype(F32)

    x_all = jnp.stack(seq.gather(x_in))
    valid = ((me * pos + jnp.arange(pos))[None, :] < lengths[:, None]).astype(F32)
    top = cotangent.astype(F32) * valid[:, :, None]
    top_all = jnp.stack(seq.gather(top.astype(BF))).reshape(ns, tok, d)

    w_qkv = collect(pick(qkv_weight, qgroups, qwidth))
    if spread:
        w_out = collect(pick_rows(out_weight))
    else:
        w_out = lax.dynamic_slice_in_dim(collect(out_weight), me * mine * HEAD_DIM, mine * HEAD_DIM, 0)
    w_down = collect(pick_rows(down_weight))
    w_gate = collect(pick(gate_weight, nf, unit))
    w_up = collect(pick(up_weight, nf, unit))

    places = jnp.stack([seq.place(j) for j in range(ns)])
    spots = places[:, None] * pos + jnp.arange(pos)[None, :]
    inverse = ROPE_BASE ** (-(jnp.arange(ROT // 2).astype(F32) * 2.0) / ROT)
    angle = jnp.arange(ns * pos).astype(F32)[:, None] * inverse
    cosine, sine = jnp.cos(angle)[:, None, :], jnp.sin(angle)[:, None, :]

    def to_positions(v):
        v = jnp.take(v.reshape(ns, slots, pos, -1), jnp.argsort(places), axis=0)
        return jnp.swapaxes(v, 0, 1).reshape(slots, ns * pos, -1)

    def from_positions(v):
        v = jnp.swapaxes(v.reshape(slots, ns, pos, -1), 0, 1)
        return jnp.take(v, places, axis=0).reshape(ns, tok, -1)

    normed = norm_stats(x_all.astype(F32))[0] * gain1 + bias1
    normed = normed.astype(BF).reshape(ns * tok, d)
    projected = to_positions(dot(normed, w_qkv, 1, 0) + bias_q).reshape(slots, ns * pos, 3, mine, HEAD_DIM)
    kept, merged = [], []
    for i in range(slots):
        q = rope(projected[i, :, 0], cosine, sine).astype(BF)
        k = rope(projected[i, :, 1], cosine, sine).astype(BF)
        v = projected[i, :, 2].astype(BF)
        out, lses = attend(q, k, v, lengths[i])
        kept.append((q, k, v, lses))
        merged.append(out.reshape(ns * pos, mine * HEAD_DIM).astype(BF))
    merged = from_positions(jnp.stack(merged))
    x_own = x_in.reshape(tok, d).astype(F32)
    residual = x_own + seq.scatter(lambda j: dot(merged[j], w_out, 1, 0))
    hat2, rstd2 = norm_stats(residual)
    two = jnp.stack(seq.gather((hat2 * gain2 + bias2).astype(BF))).reshape(ns * tok, d)
    gate_val = dot(two, w_gate, 1, 0)
    up_val = dot(two, w_up, 1, 0)
    grad_hidden = dot(top_all.reshape(ns * tok, d), w_down, 1, 1)
    sig = jax.nn.sigmoid(gate_val)
    silu = gate_val * sig
    hidden = (silu * up_val).astype(BF)
    g_gate = (grad_hidden * up_val * (sig * (1.0 + gate_val * (1.0 - sig)))).astype(BF)
    g_up = (grad_hidden * silu).astype(BF)
    gg, gu = g_gate.reshape(ns, tok, -1), g_up.reshape(ns, tok, -1)
    grad_two = seq.scatter(lambda j: dot(gg[j], w_gate, 1, 1) + dot(gu[j], w_up, 1, 1))
    hid = hidden.reshape(ns, tok, -1)
    layer_output = (residual + seq.scatter(lambda j: dot(hid[j], w_down, 1, 0))).astype(BF)
    grad_residual = top.reshape(tok, d) + norm_back(grad_two, hat2, rstd2, gain2)
    g_gain2 = jnp.sum(grad_two * hat2, axis=0)
    g_bias2 = jnp.sum(grad_two, axis=0)
    branch = jnp.stack(seq.gather(grad_residual.astype(BF))).reshape(ns * tok, d)

    gw_down = dot(hidden, top_all.reshape(ns * tok, d), 0, 0).astype(BF)
    gw_gate = dot(two, g_gate, 0, 0).astype(BF)
    gw_up = dot(two, g_up, 0, 0).astype(BF)

    grad_att = to_positions(dot(branch, w_out, 1, 1).astype(BF)).reshape(slots, ns * pos, mine, HEAD_DIM)
    grads = []
    for i in range(slots):
        q, k, v, lses = kept[i]
        dq, dk, dv = attend_back(q, k, v, lengths[i], lses, grad_att[i])
        dq, dk, dv = (t.astype(BF).astype(F32) for t in (dq, dk, dv))
        grads.append(jnp.stack([rope(dq, cosine, -sine), rope(dk, cosine, -sine), dv], axis=1).astype(BF))
    g_proj = from_positions(jnp.stack(grads))
    grad_normed = seq.scatter(lambda j: dot(g_proj[j], w_qkv, 1, 1))
    g_flat = g_proj.reshape(ns * tok, -1)
    hat1, rstd1 = norm_stats(x_own)
    grad_x = grad_residual + norm_back(grad_normed, hat1, rstd1, gain1)
    g_gain1 = jnp.sum(grad_normed * hat1, axis=0)
    g_bias1 = jnp.sum(grad_normed, axis=0)
    gw_out = dot(merged.reshape(ns * tok, -1), branch, 0, 0).astype(BF)
    gw_qkv = dot(normed, g_flat, 0, 0).astype(BF)
    g_bias_q = jnp.sum(g_flat.astype(F32), axis=0)
    own = jnp.arange(ns)[:, None, None] == me
    g_bias_q = unpick(jnp.where(own, g_bias_q[None, None, :], 0.0), qgroups, qwidth)[0]

    packed = jnp.concatenate([v.reshape(nf, -1) for v in (g_gain1, g_bias1, g_gain2, g_bias2, g_bias_q)], axis=1)
    packed = lax.psum(lax.psum_scatter(packed, "fsdp", scatter_dimension=0), "seq")
    g_ln = [packed[i * rows : (i + 1) * rows] for i in range(4)]

    def place_cols(v, groups, width):
        return unpick(seq.gather_placed(reduce(v)), groups, width).astype(F32)

    def place_rows(v):
        return seq.gather_placed(reduce(v)).reshape(-1, d).astype(F32)

    if spread:
        out_grad = place_rows(gw_out)
    else:
        full = lax.dynamic_update_slice_in_dim(jnp.zeros((heads * HEAD_DIM, d), BF), gw_out, me * mine * HEAD_DIM, 0)
        out_grad = lax.psum(reduce(full), "seq").astype(F32)
    return (
        layer_output.reshape(slots, pos, d),
        grad_x.reshape(slots, pos, d),
        g_ln[0],
        g_ln[1],
        place_cols(gw_qkv, qgroups, qwidth),
        packed[4 * rows :],
        out_grad,
        g_ln[2],
        g_ln[3],
        place_cols(gw_gate, nf, unit),
        place_cols(gw_up, nf, unit),
        place_rows(gw_down),
    )


def solution(mesh):
    tokens, vector, matrix = P("fsdp", "seq", None), P("fsdp"), P("fsdp", None)
    return jax.shard_map(
        body,
        mesh=mesh,
        in_specs=(
            tokens, vector, vector, vector, matrix, vector, matrix,
            vector, vector, matrix, matrix, matrix, tokens,
        ),
        out_specs=(
            tokens, tokens, vector, vector, matrix, vector, matrix,
            vector, vector, matrix, matrix, matrix,
        ),
        check_vma=False,
    )
```

```python
import jax
import jax.numpy as jnp
from jax import lax
from jax.experimental import pallas as pl
from jax.experimental.pallas import tpu as pltpu
from jax.sharding import PartitionSpec as P

HEAD_DIM = 64
ROT = 16
PAIR = 2 * HEAD_DIM
EPS_NORM = 1e-05
ROPE_BASE = 10000.0
NEG_FILL = -1e30
BF = jnp.bfloat16
F32 = jnp.float32


def dot(a, b, ca, cb):
    return lax.dot_general(a, b, (((ca,), (cb,)), ((), ())), preferred_element_type=F32)


def norm_stats(v):
    center = v - jnp.mean(v, axis=-1, keepdims=True)
    rstd = lax.rsqrt(jnp.mean(center * center, axis=-1, keepdims=True) + EPS_NORM)
    return center * rstd, rstd


def norm_back(grad, xhat, rstd, gain):
    gx = grad * gain
    m1 = jnp.mean(gx, axis=-1, keepdims=True)
    m2 = jnp.mean(gx * xhat, axis=-1, keepdims=True)
    return (gx - m1 - xhat * m2) * rstd


class SeqGroup:
    def __init__(self, size):
        self.size = size
        self.me = lax.axis_index("seq")
        self.offsets = (0, 2, 1, 3) if size == 4 else tuple(range(size))

    def place(self, j):
        return self.me ^ self.offsets[j] if self.size == 4 else jnp.int32(j)

    def swap(self, v, bit):
        return lax.ppermute(v, "seq", [(i, i ^ bit) for i in range(self.size)])

    def gather(self, v):
        if self.size != 4:
            return list(lax.all_gather(v, "seq", axis=0))
        far = self.swap(v, 2)
        return [v, far, self.swap(v, 1), self.swap(far, 1)]

    def scatter(self, part):
        if self.size != 4:
            terms = jnp.stack([part(j).astype(BF) for j in range(self.size)])
            return lax.psum_scatter(terms, "seq", scatter_dimension=0).astype(F32)
        diag = self.swap(part(3).astype(BF), 1)
        far = self.swap((part(1) + diag.astype(F32)).astype(BF), 2)
        near = self.swap(part(2).astype(BF), 1)
        return part(0) + near.astype(F32) + far.astype(F32)

    def gather_placed(self, v):
        blocks = self.gather(v)
        if self.size != 4:
            return jnp.stack(blocks)
        low = (self.me & 1) == 0
        high = (self.me & 2) == 0
        a, c, b, d = blocks
        first = [jnp.where(low, a, b), jnp.where(low, b, a)]
        second = [jnp.where(low, c, d), jnp.where(low, d, c)]
        return jnp.stack(
            [jnp.where(high, x, y) for x, y in zip(first, second)]
            + [jnp.where(high, y, x) for x, y in zip(first, second)]
        )


def wheel(n):
    h = ROT // 2
    inverse = ROPE_BASE ** (-(jnp.arange(h).astype(F32) * 2.0) / ROT)
    angle = jnp.arange(n).astype(F32)[:, None] * inverse[None, :]
    c, s = jnp.cos(angle), jnp.sin(angle)
    one, nil = jnp.ones((n, HEAD_DIM - ROT), F32), jnp.zeros((n, HEAD_DIM - ROT), F32)
    none = jnp.zeros((n, h), F32)
    own = jnp.concatenate([c, c, one], axis=1)
    ahead = jnp.concatenate([-s, none, nil], axis=1)
    behind = jnp.concatenate([none, s, nil], axis=1)
    return jnp.stack([jnp.tile(t, (1, 2)) for t in (own, ahead, behind)])


def turn(v, tab, rows, sign):
    h = ROT // 2
    ahead = pltpu.roll(v, PAIR - h, 1) * tab[1, rows, :]
    behind = pltpu.roll(v, h, 1) * tab[2, rows, :]
    return v * tab[0, rows, :] + sign * (ahead + behind)


def load_turned(place_ref, tab_ref, q_ref, k_ref, v_ref, q_s, k_s, v_s):
    ns, pos = q_ref.shape[0], q_ref.shape[2]
    for j in range(ns):
        rows = pl.ds(pl.multiple_of(place_ref[j] * pos, pos), pos)
        q = turn(q_ref[j, 0].astype(F32), tab_ref, rows, 1.0) * HEAD_DIM**-0.5
        k_s[rows, :] = turn(k_ref[j, 0].astype(F32), tab_ref, rows, 1.0).astype(BF)
        q_s[rows, :] = q.astype(BF)
        v_s[rows, :] = v_ref[j, 0]


def head_lanes(v, h):
    lane = lax.broadcasted_iota(jnp.int32, v.shape, 1)
    return jnp.where((lane < HEAD_DIM) == (h == 0), v, jnp.zeros_like(v))


def key_major(a, b):
    return dot(a, b, 1, 1)


def masked(sc, first, p, pos, limit):
    key = lax.broadcasted_iota(jnp.int32, sc.shape, 0)
    if first == p * pos:
        query = lax.broadcasted_iota(jnp.int32, sc.shape, 1)
        return jnp.where((key <= query) & (key < limit - first), sc, NEG_FILL)
    return jnp.where(key < limit - first, sc, NEG_FILL)


def spans(p, pos):
    return ([(0, p * pos)] if p else []) + [(p * pos, pos)]


def fwd_kernel(place_ref, len_ref, tab_ref, q_ref, k_ref, v_ref, o_ref, lse_ref, q_s, k_s, v_s, vt_s):
    ns, pos = q_ref.shape[0], q_ref.shape[2]
    limit = len_ref[pl.program_id(0)]
    load_turned(place_ref, tab_ref, q_ref, k_ref, v_ref, q_s, k_s, v_s)
    vt_s[...] = v_s[...].T
    for p in range(ns):
        q = q_s[p * pos : (p + 1) * pos, :]
        halves = []
        for h in range(2):
            qh = head_lanes(q, h)
            sc = [masked(key_major(k_s[a : a + n, :], qh), a, p, pos, limit) for a, n in spans(p, pos)]
            peak = jnp.max(sc[0], axis=0, keepdims=True)
            if p:
                peak = jnp.maximum(peak, jnp.max(sc[1], axis=0, keepdims=True))
            total, acc = 0.0, 0.0
            for (a, n), t in zip(spans(p, pos), sc):
                e = jnp.exp(t - peak)
                total = total + jnp.sum(e, axis=0, keepdims=True)
                acc = acc + dot(vt_s[h * HEAD_DIM : (h + 1) * HEAD_DIM, a : a + n], e.astype(BF), 1, 0)
            halves.append(acc / total)
            lse_ref[0, 0, h : h + 1, p * pos : (p + 1) * pos] = peak + jnp.log(total)
        o_ref[place_ref[ns + p], 0] = jnp.concatenate(halves, axis=0).T.astype(BF)


def bwd_kernel(place_ref, len_ref, tab_ref, q_ref, k_ref, v_ref, lse_ref, g_ref, d_ref, q_s, k_s, v_s, kt_s, dk_s, dv_s):
    ns, pos = q_ref.shape[0], q_ref.shape[2]
    pair, width = pl.program_id(1), d_ref.shape[3] // 3
    limit = len_ref[pl.program_id(0)]
    load_turned(place_ref, tab_ref, q_ref, k_ref, v_ref, q_s, k_s, v_s)
    kt_s[...] = k_s[...].T
    dk_s[...] = jnp.zeros_like(dk_s)
    dv_s[...] = jnp.zeros_like(dv_s)

    def columns(part):
        return pl.ds(pl.multiple_of(part * width + pair * PAIR, PAIR), PAIR)

    for p in range(ns):
        j = place_ref[ns + p]
        mine = slice(p * pos, (p + 1) * pos)

        @pl.when(p * pos >= limit)
        def _():
            d_ref[j, 0, :, columns(0)] = jnp.zeros((pos, PAIR), BF)

        @pl.when(p * pos < limit)
        def _():
            q = q_s[mine, :]
            g = g_ref[j, 0]
            halves = []
            for h in range(2):
                qh, gh = head_lanes(q, h), head_lanes(g, h)
                lse = lse_ref[0, 0, h : h + 1, mine]
                prob, grad, delta = [], [], 0.0
                for a, n in spans(p, pos):
                    e = jnp.exp(masked(key_major(k_s[a : a + n, :], qh), a, p, pos, limit) - lse)
                    gp = key_major(v_s[a : a + n, :], gh)
                    delta = delta + jnp.sum(e * gp, axis=0, keepdims=True)
                    prob.append(e)
                    grad.append(gp)
                acc = 0.0
                for (a, n), e, gp in zip(spans(p, pos), prob, grad):
                    ds = (e * (gp - delta)).astype(BF)
                    dk_s[a : a + n, :] += dot(ds, qh, 1, 0)
                    dv_s[a : a + n, :] += dot(e.astype(BF), gh, 1, 0)
                    acc = acc + dot(kt_s[h * HEAD_DIM : (h + 1) * HEAD_DIM, a : a + n], ds, 1, 0)
                halves.append(acc)
            dq = jnp.concatenate(halves, axis=0).T * HEAD_DIM**-0.5
            d_ref[j, 0, :, columns(0)] = turn(dq, tab_ref, slice(p * pos, (p + 1) * pos), -1.0).astype(BF)

    for p in range(ns):
        j = place_ref[ns + p]
        mine = slice(p * pos, (p + 1) * pos)
        d_ref[j, 0, :, columns(1)] = turn(dk_s[mine, :], tab_ref, mine, -1.0).astype(BF)
        d_ref[j, 0, :, columns(2)] = dv_s[mine, :].astype(BF)


def attention_specs(ns, slots, pos, width):
    pairs = width // PAIR
    column = lambda part: pl.BlockSpec((ns, 1, pos, PAIR), lambda b, h, *_: (0, b, 0, part * pairs + h))
    table = pl.BlockSpec((3, ns * pos, PAIR), lambda b, h, *_: (0, 0, 0))
    lse = pl.BlockSpec((1, 1, 2, ns * pos), lambda b, h, *_: (b, h, 0, 0))
    return (slots, pairs), column, table, lse


def attend(place, lengths, tab, proj):
    ns, slots, pos, width = proj.shape
    width //= 3
    grid, column, table, lse = attention_specs(ns, slots, pos, width)
    n = ns * pos
    return pl.pallas_call(
        fwd_kernel,
        grid_spec=pltpu.PrefetchScalarGridSpec(
            num_scalar_prefetch=2,
            grid=grid,
            in_specs=[table, column(0), column(1), column(2)],
            out_specs=[column(0), lse],
            scratch_shapes=[pltpu.VMEM((n, PAIR), BF)] * 3 + [pltpu.VMEM((PAIR, n), BF)],
        ),
        out_shape=[
            jax.ShapeDtypeStruct((ns, slots, pos, width), BF),
            jax.ShapeDtypeStruct((slots, width // PAIR, 2, n), F32),
        ],
        cost_estimate=pl.CostEstimate(
            flops=4 * slots * n * n * width, bytes_accessed=8 * slots * n * width, transcendentals=slots * n * n * width // 128
        ),
        name="attend",
    )(place, lengths, tab, proj, proj, proj)


def attend_back(place, lengths, tab, proj, lse_in, grad):
    ns, slots, pos, width = grad.shape
    grid, column, table, lse = attention_specs(ns, slots, pos, width)
    n = ns * pos
    return pl.pallas_call(
        bwd_kernel,
        grid_spec=pltpu.PrefetchScalarGridSpec(
            num_scalar_prefetch=2,
            grid=grid,
            in_specs=[table, column(0), column(1), column(2), lse, column(0)],
            out_specs=pl.BlockSpec((ns, 1, pos, 3 * width), lambda b, h, *_: (0, b, 0, 0)),
            scratch_shapes=[pltpu.VMEM((n, PAIR), BF)] * 3
            + [pltpu.VMEM((PAIR, n), BF)]
            + [pltpu.VMEM((n, PAIR), F32)] * 2,
        ),
        out_shape=jax.ShapeDtypeStruct((ns, slots, pos, 3 * width), BF),
        cost_estimate=pl.CostEstimate(
            flops=10 * slots * n * n * width, bytes_accessed=14 * slots * n * width, transcendentals=slots * n * n * width // 128
        ),
        name="attend_back",
    )(place, lengths, tab, proj, proj, proj, lse_in, grad)


def body(
    x_in, lengths, ln1_gain, ln1_bias, qkv_weight, qkv_bias, out_weight,
    ln2_gain, ln2_bias, gate_weight, up_weight, down_weight, cotangent,
):
    nf, ns = lax.axis_size("fsdp"), lax.axis_size("seq")
    seq = SeqGroup(ns)
    me = seq.me
    slots, pos, d = x_in.shape
    rows = qkv_weight.shape[0]
    heads = qkv_weight.shape[1] // (3 * HEAD_DIM)
    mine = heads // ns
    tok = slots * pos
    ff = gate_weight.shape[1]
    unit = ff // (nf * ns)
    spread = (heads // nf) % ns == 0

    def pick(v, groups, width):
        v = v.reshape(v.shape[0], groups, ns, width)
        v = lax.dynamic_index_in_dim(v, me, axis=2, keepdims=False)
        return v.reshape(v.shape[0], groups * width)

    def unpick(pieces, groups, width):
        v = pieces.reshape(ns, pieces.shape[1], groups, width)
        return jnp.moveaxis(v, 0, 2).reshape(pieces.shape[1], groups * ns * width)

    def pick_rows(v):
        return lax.dynamic_index_in_dim(v.reshape(ns, v.shape[0] // ns, v.shape[1]), me, 0, keepdims=False)

    ny = 2 if nf == 8 else 1
    nz = nf // ny
    y = lax.axis_index("fsdp") % ny
    along_z = [[z * ny + i for z in range(nz)] for i in range(ny)]
    swap_y = [(i, i ^ 1) for i in range(nf)]

    def collect(v):
        if ny == 1:
            return lax.all_gather(v, "fsdp", axis=0, tiled=True)
        own = lax.all_gather(v, "fsdp", axis=0, axis_index_groups=along_z)
        other = lax.ppermute(own, "fsdp", swap_y)
        first, second = jnp.where(y == 0, own, other), jnp.where(y == 0, other, own)
        return jnp.stack([first, second], axis=1).reshape(nf * v.shape[0], v.shape[1])

    def reduce(v):
        if ny == 1:
            return lax.psum_scatter(v, "fsdp", scatter_dimension=0, tiled=True)
        v = v.reshape(nz, ny, v.shape[0] // nf, v.shape[1])
        other = lax.dynamic_index_in_dim(v, 1 - y, 1, keepdims=False)
        own = lax.dynamic_index_in_dim(v, y, 1, keepdims=False)
        own = (own.astype(F32) + lax.ppermute(other, "fsdp", swap_y).astype(F32)).astype(BF)
        return lax.psum_scatter(own, "fsdp", scatter_dimension=0, axis_index_groups=along_z)

    qgroups, qwidth = (3 * nf, mine * HEAD_DIM // nf) if spread else (3, mine * HEAD_DIM)

    small = lax.all_gather(jnp.concatenate([ln1_gain, ln1_bias, ln2_gain, ln2_bias, qkv_bias]), "fsdp", axis=0)
    gain1, bias1, gain2, bias2 = (small[:, i * rows : (i + 1) * rows].reshape(d).astype(F32) for i in range(4))
    bias_q = pick(small[:, 4 * rows :].reshape(1, -1), qgroups, qwidth).astype(F32)

    x_all = jnp.stack(seq.gather(x_in))
    valid = ((me * pos + jnp.arange(pos))[None, :] < lengths[:, None]).astype(F32)
    top = cotangent.astype(F32) * valid[:, :, None]
    top_all = jnp.stack(seq.gather(top.astype(BF))).reshape(ns, tok, d)

    w_qkv = lax.all_gather(pick(qkv_weight, qgroups, qwidth), "fsdp", axis=0, tiled=True)
    if spread:
        w_out = collect(pick_rows(out_weight))
    else:
        w_out = lax.dynamic_slice_in_dim(collect(out_weight), me * mine * HEAD_DIM, mine * HEAD_DIM, 0)
    w_down = collect(pick_rows(down_weight))
    w_gate = collect(pick(gate_weight, nf, unit))
    w_up = collect(pick(up_weight, nf, unit))

    places = jnp.stack([seq.place(j) for j in range(ns)])
    order = jnp.concatenate([places, jnp.argsort(places)]).astype(jnp.int32)
    tab = wheel(ns * pos)

    normed = norm_stats(x_all.astype(F32))[0] * gain1 + bias1
    normed = normed.astype(BF).reshape(ns * tok, d)
    normed, top_all = lax.optimization_barrier((normed, top_all))
    projected = (dot(normed, w_qkv, 1, 0) + bias_q).astype(BF).reshape(ns, slots, pos, -1)
    merged, lse = attend(order, lengths, tab, projected)
    merged = merged.reshape(ns, tok, -1)
    x_own = x_in.reshape(tok, d).astype(F32)
    residual = x_own + seq.scatter(lambda j: dot(merged[j], w_out, 1, 0))
    hat2, rstd2 = norm_stats(residual)
    two = jnp.stack(seq.gather((hat2 * gain2 + bias2).astype(BF))).reshape(ns * tok, d)
    gate_val = dot(two, w_gate, 1, 0)
    up_val = dot(two, w_up, 1, 0)
    grad_hidden = dot(top_all.reshape(ns * tok, d), w_down, 1, 1)
    sig = jax.nn.sigmoid(gate_val)
    silu = gate_val * sig
    hidden = (silu * up_val).astype(BF)
    g_gate = (grad_hidden * up_val * (sig * (1.0 + gate_val * (1.0 - sig)))).astype(BF)
    g_up = (grad_hidden * silu).astype(BF)
    gg, gu = g_gate.reshape(ns, tok, -1), g_up.reshape(ns, tok, -1)
    grad_two = seq.scatter(lambda j: dot(gg[j], w_gate, 1, 1) + dot(gu[j], w_up, 1, 1))
    grad_residual = top.reshape(tok, d) + norm_back(grad_two, hat2, rstd2, gain2)
    g_gain2 = jnp.sum(grad_two * hat2, axis=0)
    g_bias2 = jnp.sum(grad_two, axis=0)
    branch = jnp.stack(seq.gather(grad_residual.astype(BF))).reshape(ns * tok, d)

    hid, branch = lax.optimization_barrier((hidden.reshape(ns, tok, -1), branch))
    layer_output = (residual + seq.scatter(lambda j: dot(hid[j], w_down, 1, 0))).astype(BF)

    gw_down = dot(hidden, top_all.reshape(ns * tok, d), 0, 0).astype(BF)
    gw_gate = dot(two, g_gate, 0, 0).astype(BF)
    gw_up = dot(two, g_up, 0, 0).astype(BF)

    grad_att = dot(branch, w_out, 1, 1).astype(BF).reshape(ns, slots, pos, -1)
    g_proj = attend_back(order, lengths, tab, projected, lse, grad_att).reshape(ns, tok, -1)
    grad_normed = seq.scatter(lambda j: dot(g_proj[j], w_qkv, 1, 1))
    g_flat = g_proj.reshape(ns * tok, -1)
    hat1, rstd1 = norm_stats(x_own)
    grad_x = grad_residual + norm_back(grad_normed, hat1, rstd1, gain1)
    g_gain1 = jnp.sum(grad_normed * hat1, axis=0)
    g_bias1 = jnp.sum(grad_normed, axis=0)
    gw_out = dot(merged.reshape(ns * tok, -1), branch, 0, 0).astype(BF)
    gw_qkv = dot(normed, g_flat, 0, 0).astype(BF)
    g_bias_q = jnp.sum(g_flat.astype(F32), axis=0)
    own = jnp.arange(ns)[:, None, None] == me
    g_bias_q = unpick(jnp.where(own, g_bias_q[None, None, :], 0.0), qgroups, qwidth)[0]

    packed = jnp.concatenate([v.reshape(nf, -1) for v in (g_gain1, g_bias1, g_gain2, g_bias2, g_bias_q)], axis=1)
    packed = lax.psum(lax.psum_scatter(packed, "fsdp", scatter_dimension=0), "seq")
    g_ln = [packed[i * rows : (i + 1) * rows] for i in range(4)]

    def place_cols(v, groups, width):
        return unpick(seq.gather_placed(reduce(v)), groups, width).astype(F32)

    def place_rows(v):
        return seq.gather_placed(reduce(v)).reshape(-1, d).astype(F32)

    if spread:
        out_grad = place_rows(gw_out)
    else:
        full = lax.dynamic_update_slice_in_dim(jnp.zeros((heads * HEAD_DIM, d), BF), gw_out, me * mine * HEAD_DIM, 0)
        out_grad = lax.psum(reduce(full), "seq").astype(F32)
    return (
        layer_output.reshape(slots, pos, d),
        grad_x.reshape(slots, pos, d),
        g_ln[0],
        g_ln[1],
        place_cols(gw_qkv, qgroups, qwidth),
        packed[4 * rows :],
        out_grad,
        g_ln[2],
        g_ln[3],
        place_cols(gw_gate, nf, unit),
        place_cols(gw_up, nf, unit),
        place_rows(gw_down),
    )


def solution(mesh):
    tokens, vector, matrix = P("fsdp", "seq", None), P("fsdp"), P("fsdp", None)
    return jax.shard_map(
        body,
        mesh=mesh,
        in_specs=(
            tokens, vector, vector, vector, matrix, vector, matrix,
            vector, vector, matrix, matrix, matrix, tokens,
        ),
        out_specs=(
            tokens, tokens, vector, vector, matrix, vector, matrix,
            vector, vector, matrix, matrix, matrix,
        ),
        check_vma=False,
    )
```
